128 devices in a mesh: dp: 16 (over y, x), expert: 8 (over z, core).
Axes of the slice: x: 4, y: 4, z: 4, core: 2. Of those that a mesh axis runs over, the one named last changes fastest.
Arguments:
- tokens: bfloat16 [2048, 2048], P(('dp', 'expert')), may hold values from -6 to 6
- route: int32 [2048, 8], P(('dp', 'expert')), may hold values from 0 to 63, all different within a row; in each aligned block of 16 rows (0 to 15, 16 to 31, ...) at most 2 rows name the same one
- probs: float32 [2048, 8], P(('dp', 'expert')), may hold values from 0.03 to 0.3
- cotangent: bfloat16 [2048, 2048], P(('dp', 'expert')), may hold values from -6 to 6
- gate_weight: bfloat16 [128, 2048, 384], P(('dp', 'expert')), may hold values from -0.125 to 0.125
- up_weight: bfloat16 [128, 2048, 384], P(('dp', 'expert')), may hold values from -0.125 to 0.125
- down_weight: bfloat16 [128, 384, 2048], P(('dp', 'expert')), may hold values from -0.21875 to 0.21875
Outputs:
- mixed: bfloat16 [2048, 2048], P(('dp', 'expert'))
- token_grad: bfloat16 [2048, 2048], P(('dp', 'expert'))
- gate_grad: bfloat16 [128, 2048, 384], P(('dp', 'expert'))
- up_grad: bfloat16 [128, 2048, 384], P(('dp', 'expert'))
- down_grad: bfloat16 [128, 384, 2048], P(('dp', 'expert'))
The draws below stay inside these ranges and needn't reach their ends.
Inputs may be any that keep to these rules, and one draw needn't show every extreme that they name: `route`: each row names 8 different experts. In each aligned block of 16 rows (the rows of one device) no expert is named by more than 2 rows, a bound that some block reaches.
All inputs are finite; a program needn't handle non-finite values.
Results may differ from the reference program's by a relative error of at most 0.0065.
Values may be sent and summed in bfloat16 or wider, within the bound.
A program may use at most 64 MiB of HBM per device.

```python
import math
import jax
import jax.numpy as jnp
import numpy as np
from jax import lax

D = 2048
HID = 768
TOP = 8
TOK_DEV = 16
DEVICES_ALL = 128
EXPERTS = 64
HSLICE = 384
CAP = 2
TOKENS = 2048
N_DP = 16
N_EXPERT = 8


def steps_of(key, extent, split, smallest, high):
    loudness = 1.0
    for dim, parts in split:
        steps = jax.random.uniform(jax.random.fold_in(jax.random.fold_in(key, 6), dim), (parts,), jnp.float32, smallest / len(split), high / len(split))
        loudness = loudness * jnp.repeat(jnp.exp(steps), extent[dim] // parts).reshape((-1,) + (1,) * (len(extent) - 1 - dim))
    return loudness


def deal_out(own_key, own, number, rows, number_of, top, limit, slope):
    order = jax.random.permutation(own_key, number_of)
    packed, common = load_shares(number_of, rows * top, limit, slope, True), load_shares(number_of, rows * top, limit, slope, False)
    places = jnp.arange(number_of)

    def named(lengths, turn):
        used = int((lengths > 0).sum())
        fixed = max(1, used // 4)
        passed = fixed + (places - fixed + turn * (used - fixed)) % max(1, number_of - fixed)
        return jnp.zeros((number_of,), jnp.int32).at[order[jnp.where(places < fixed, places, passed)]].set(jnp.asarray(lengths, jnp.int32))

    lengths = jnp.where(number % 4 == 0, named(packed, number // 4), named(common, number - number // 4 - 1))
    mixed = jax.random.permutation(jax.random.fold_in(own, 3), number_of)
    donor, taker = mixed[0:number_of // 2 * 2:2], mixed[1:number_of // 2 * 2:2]
    room = jnp.minimum(lengths[donor] - 1, limit - lengths[taker]) // 2
    room = jnp.where((donor == order[0]) | (taker == order[0]) | (lengths[taker] == 0), 0, jnp.maximum(room, 0))
    passed = jax.random.randint(jax.random.fold_in(own, 4), (number_of // 2,), 0, 1 << 20) % (room + 1)
    lengths = lengths.at[donor].add(-passed).at[taker].add(passed)
    members = jnp.searchsorted(jnp.cumsum(lengths), jnp.arange(rows * top), side="right").astype(jnp.int32)
    grid = members.reshape(top, rows).T
    grid = grid[jax.random.permutation(jax.random.fold_in(own, 1), rows)]
    turn = jax.random.randint(jax.random.fold_in(own, 2), (rows, 1), 0, top)
    return jnp.take_along_axis(grid, (jnp.arange(top)[None, :] + turn) % top, axis=1)


def load_shares(number_of, total, reach, lean, full):
    portions = [(1 << 20) // math.isqrt(grade ** lean) + 1 for grade in range(1, number_of + 1)]
    largest = reach if full else min(reach, max(-(-total // number_of), total * portions[0] // sum(portions)))
    least = 1 if total - largest >= number_of - 1 else 0
    given, spare = [largest] + [least] * (number_of - 1), total - largest - least * (number_of - 1)
    while spare > 0:
        movable = [i for i in range(1, number_of) if given[i] < largest] or [i for i in range(1, number_of) if given[i] < reach]
        mass, remaining = sum([portions[i] for i in movable]), spare
        for i in movable:
            extra = min(reach - given[i], max(1, remaining * portions[i] // mass), spare)
            given[i] = given[i] + extra
            spare = spare - extra
    return np.array(given)


def noise(stream_key, shape, width, reach, cuts=(), kind=jnp.bfloat16):
    loudness = steps_of(stream_key, shape, cuts, -0.22, 0.18) if cuts else 1.0
    drawn = jax.random.normal(stream_key, shape, jnp.float32) * width * loudness
    return jnp.minimum(jnp.maximum(drawn, -reach), reach).astype(kind)


def setup_inputs(seed: int = 0) -> dict:
    key_of = jax.random.split(jax.random.key(seed), 8)
    tokens = noise(key_of[0], (TOKENS, D), 1.0, 6.0, ((0, 128),))
    route_keys = jax.random.split(jax.random.fold_in(key_of[1], 1), TOKENS // TOK_DEV)
    route_turns = jax.random.permutation(jax.random.fold_in(key_of[1], 3), TOKENS // TOK_DEV)
    route = jax.vmap(lambda own, number: deal_out(jax.random.fold_in(key_of[1], 2), own, number, TOK_DEV, EXPERTS, TOP, CAP, 2))(route_keys, route_turns).reshape((TOKENS, TOP))
    probs = jnp.clip(jnp.exp(math.log(0.3) - 2.3025852 * jax.random.uniform(key_of[2], (TOKENS, TOP), jnp.float32) ** steps_of(key_of[2], (TOKENS, TOP), ((0, 128),), -0.2, 0.2)), 0.03, 0.3)
    cotangent = noise(key_of[3], (TOKENS, D), 1.0, 6.0, ((0, 128),))
    gate_weight = noise(key_of[4], (DEVICES_ALL, D, HSLICE), D ** -0.5, 0.125, ((0, 128),))
    up_weight = noise(key_of[5], (DEVICES_ALL, D, HSLICE), D ** -0.5, 0.125, ((0, 128),))
    down_weight = noise(key_of[6], (DEVICES_ALL, HSLICE, D), HID ** -0.5, 0.21875, ((0, 128),))
    return {"tokens": tokens, "route": route, "probs": probs, "cotangent": cotangent, "gate_weight": gate_weight, "up_weight": up_weight, "down_weight": down_weight}


def slot_tables(route_block, prob_block, experts, capacity):
    row_count, top_count = route_block.shape
    flat_ids = route_block.reshape(-1)
    onehot = (flat_ids[:, None] == jnp.arange(experts, dtype=jnp.int32)[None, :]).astype(jnp.int32)
    before = jnp.cumsum(onehot, axis=0) - onehot
    position = jnp.sum(before * onehot, axis=1).astype(jnp.int32)
    slot_ids = (flat_ids * capacity + position).astype(jnp.int32)
    matches = (slot_ids[:, None] == jnp.arange(experts * capacity, dtype=jnp.int32)[None, :]).astype(jnp.float32)
    matches = matches.reshape(row_count, top_count, experts * capacity)
    return jnp.sum(matches, axis=1), jnp.sum(matches * prob_block[:, :, None].astype(jnp.float32), axis=1)


def rounded(values):
    return lax.optimization_barrier(values.astype(jnp.bfloat16)).astype(jnp.float32)


def reference(tokens, route, probs, cotangent, gate_weight, up_weight, down_weight):
    highest = lax.Precision.HIGHEST
    device_count = N_DP * N_EXPERT
    hslice = HID // 2
    gate_full = gate_weight.reshape(EXPERTS, 2, D, hslice).transpose(0, 2, 1, 3).reshape(EXPERTS, D, HID)
    up_full = up_weight.reshape(EXPERTS, 2, D, hslice).transpose(0, 2, 1, 3).reshape(EXPERTS, D, HID)
    down_full = down_weight.reshape(EXPERTS, HID, D)
    token_all = tokens.reshape(device_count, TOK_DEV, D).astype(jnp.float32)
    cot_all = cotangent.reshape(device_count, TOK_DEV, D).astype(jnp.float32)
    spread, weighted = jax.vmap(lambda a, b: slot_tables(a, b, EXPERTS, CAP))(
        route.reshape(device_count, TOK_DEV, TOP), probs.reshape(device_count, TOK_DEV, TOP))
    spread = spread.reshape(device_count, TOK_DEV, EXPERTS, CAP)
    weighted = weighted.reshape(device_count, TOK_DEV, EXPERTS, CAP)

    def one_expert(totals, index):
        spread_part = lax.dynamic_index_in_dim(spread, index, 2, keepdims=False)
        weight_part = lax.dynamic_index_in_dim(weighted, index, 2, keepdims=False)
        w_gate = lax.dynamic_index_in_dim(gate_full, index, 0, keepdims=False).astype(jnp.float32)
        w_up = lax.dynamic_index_in_dim(up_full, index, 0, keepdims=False).astype(jnp.float32)
        w_down = lax.dynamic_index_in_dim(down_full, index, 0, keepdims=False).astype(jnp.float32)
        slot_rows = rounded(jnp.einsum('ntc,ntd->ncd', spread_part, token_all, precision=highest)).reshape(-1, D)
        out_cot = rounded(jnp.einsum('ntc,ntd->ncd', weight_part, cot_all, precision=highest)).reshape(-1, D)
        gate_val = jnp.dot(slot_rows, w_gate, precision=highest)
        up_val = jnp.dot(slot_rows, w_up, precision=highest)
        sigmoid_val = jax.nn.sigmoid(gate_val)
        act_val = rounded(gate_val * sigmoid_val * up_val)
        out_rows = rounded(jnp.dot(act_val, w_down, precision=highest))
        act_cot = jnp.einsum('rd,hd->rh', out_cot, w_down, precision=highest)
        gate_cot = rounded(act_cot * up_val * sigmoid_val * (1.0 + gate_val * (1.0 - sigmoid_val)))
        up_cot = rounded(act_cot * gate_val * sigmoid_val)
        grad_down = jnp.einsum('rh,rd->hd', act_val, out_cot, precision=highest)
        grad_gate = jnp.einsum('rd,rh->dh', slot_rows, gate_cot, precision=highest)
        grad_up = jnp.einsum('rd,rh->dh', slot_rows, up_cot, precision=highest)
        rows_cot = rounded(jnp.einsum('rh,dh->rd', gate_cot, w_gate, precision=highest)
                           + jnp.einsum('rh,dh->rd', up_cot, w_up, precision=highest))
        out_rows = out_rows.reshape(device_count, CAP, D)
        rows_cot = rows_cot.reshape(device_count, CAP, D)
        mixed_acc = totals[0] + jnp.einsum('ntc,ncd->ntd', weight_part, out_rows, precision=highest)
        token_acc = totals[1] + jnp.einsum('ntc,ncd->ntd', spread_part, rows_cot, precision=highest)
        gate_slices = grad_gate.reshape(D, 2, hslice).transpose(1, 0, 2)
        up_slices = grad_up.reshape(D, 2, hslice).transpose(1, 0, 2)
        down_slices = grad_down.reshape(2, hslice, D)
        return (mixed_acc, token_acc), (gate_slices.astype(jnp.bfloat16), up_slices.astype(jnp.bfloat16),
                                        down_slices.astype(jnp.bfloat16))

    zeros = jnp.zeros((device_count, TOK_DEV, D), jnp.float32)
    (mixed_acc, token_acc), grads = lax.scan(one_expert, (zeros, zeros), jnp.arange(EXPERTS, dtype=jnp.int32))
    mixed = mixed_acc.reshape(TOKENS, D).astype(jnp.bfloat16)
    token_grad = token_acc.reshape(TOKENS, D).astype(jnp.bfloat16)
    gate_grad = grads[0].reshape(device_count, D, hslice)
    up_grad = grads[1].reshape(device_count, D, hslice)
    down_grad = grads[2].reshape(device_count, hslice, D)
    return mixed, token_grad, gate_grad, up_grad, down_grad
```

```python
import functools

import jax
import jax.numpy as jnp
from jax import lax
from jax.experimental import pallas as pl
from jax.experimental.pallas import tpu as pltpu
from jax.sharding import PartitionSpec as P


BF = jnp.bfloat16
F32 = jnp.float32
MESH = pl.DeviceIdType.MESH
GROUPS = (1, 3, 0, 2)


def dot(a, b):
    return jnp.dot(a, b, preferred_element_type=F32)


def dot_nt(a, b):
    return lax.dot_general(a, b, (((1,), (1,)), ((), ())), preferred_element_type=F32)


def dot_tn(a, b):
    return lax.dot_general(a, b, (((0,), (0,)), ((), ())), preferred_element_type=F32)


def iota(shape, dim):
    return lax.broadcasted_iota(jnp.int32, shape, dim)


def exchange(
    route_h, probs_h, tok_h, cot_h, wg_h, wu_h, wd_h,
    back, sel_t, g_gate, g_up, g_down,
    route_v, probs_v, tok_v, cot_v, wgu, wd, perm, perm_t, sel, parts, send, got,
    got_other, xt, xc, act, gu, mine, theirs, given, summed, ret,
    hsem, ss, rs, lsem, ps, pr,
):
    dp, ex = lax.axis_index("dp"), lax.axis_index("expert")
    x, y, z, c = lax.rem(dp, 4), dp // 4, ex // 2, lax.rem(ex, 2)

    def device(dx, dy, dz):
        return (
            lax.rem(y + dy + 4, 4) * 4 + lax.rem(x + dx + 4, 4),
            lax.rem(z + dz + 4, 4) * 2 + c,
        )

    def chip(dx, dy, dz):
        return (
            lax.rem(y + dy + 4, 4) * 16
            + lax.rem(x + dx + 4, 4) * 4
            + lax.rem(z + dz + 4, 4)
        )

    other = (dp, z * 2 + 1 - c)
    me = chip(0, 0, 0)

    barrier = pltpu.get_barrier_semaphore()

    def far(v):
        return lax.rem(2 + v, 4) + (v // 2) * (1 - 2 * lax.rem(v, 2))

    def greet(i, carry):
        there = device(far(lax.rem(i, 4)), far(lax.rem(i // 4, 4)), far(i // 16))
        pl.semaphore_signal(barrier, 1, device_id=there, device_id_type=MESH)
        return carry

    lax.fori_loop(0, 63, greet, 0)
    pl.semaphore_signal(barrier, 1, device_id=other, device_id_type=MESH)

    loads = [
        pltpu.make_async_copy(route_h, route_v, hsem.at[0]),
        pltpu.make_async_copy(probs_h, probs_v, hsem.at[1]),
        pltpu.make_async_copy(tok_h, tok_v, hsem.at[2]),
        pltpu.make_async_copy(cot_h, cot_v, hsem.at[3]),
        pltpu.make_async_copy(wg_h.at[0], wgu.at[:, pl.ds(0, 384)], hsem.at[4]),
        pltpu.make_async_copy(wu_h.at[0], wgu.at[:, pl.ds(384, 384)], hsem.at[5]),
        pltpu.make_async_copy(wd_h.at[0], wd, hsem.at[6]),
    ]
    for load in loads:
        load.start()

    def where_from(o):
        return (o // 2 % 16) * 16 + (o // 64) * 4 + (o // 32 % 2) * 2 + o % 2

    rows, cols = iota((256, 256), 0), iota((256, 256), 1)
    perm[...] = jnp.where(cols == where_from(rows), 1.0, 0.0).astype(BF)
    perm_t[...] = jnp.where(rows == where_from(cols), 1.0, 0.0).astype(BF)

    loads[0].wait()
    loads[1].wait()
    route, probs = route_v[...], probs_v[...]
    lane = iota((16, 128), 1)
    hits = jnp.zeros((16, 128), F32)
    weights = jnp.zeros((16, 128), F32)
    for k in range(8):
        same = route[:, k : k + 1] == lane % 64
        hits = hits + jnp.where(same, 1.0, 0.0)
        weights = weights + jnp.where(same, probs[:, k : k + 1], 0.0)
    earlier = jnp.where(iota((16, 16), 1) < iota((16, 16), 0), 1.0, 0.0).astype(BF)
    before = dot(earlier, hits.astype(BF)).astype(jnp.int32)
    slot = jnp.where(before == lane // 64, hits, 0.0)
    weights = weights * slot
    high = weights.astype(BF)
    rest = weights - high.astype(F32)
    middle = rest.astype(BF)
    low = (rest - middle.astype(F32)).astype(BF)
    spread = jnp.concatenate([slot.astype(BF), high, middle, low] * 4, axis=0)

    loads[2].wait()
    loads[3].wait()
    for q in range(4):
        quarter = slice(q * 512, (q + 1) * 512)
        parts[q * 64 : q * 64 + 16, :] = tok_v[:, quarter]
        for a in range(1, 4):
            parts[q * 64 + a * 16 : q * 64 + a * 16 + 16, :] = cot_v[:, quarter]

    for block in range(4):
        row = iota((256, 128), 0) + block * 256
        lane = iota((256, 128), 1)
        place = (row // 16 == lane % 64) & (row % 2 == lane // 64)
        picked = dot_nt(jnp.where(place, 1.0, 0.0).astype(BF), spread)
        row, col = iota((256, 256), 0), iota((256, 256), 1)
        right = (row // 4 % 4 == col // 64) & (
            (row // 2 % 2 == 1) == (col // 16 % 4 != 0)
        )
        picked = jnp.where(right, picked, 0.0)
        here = slice(block * 256, (block + 1) * 256)
        sel[here, :] = picked.astype(BF)
        send[here, :] = dot(sel[here, :], parts[...]).astype(BF)
        sel_t[:, here] = picked.T.astype(BF)

    pl.semaphore_wait(barrier, 64)

    def out_unit(group, i, sem):
        d = (i // 4, GROUPS[group], lax.rem(i, 4))
        pltpu.make_async_remote_copy(
            send.at[pl.ds(pl.multiple_of(chip(*d) * 16, 16), 16)],
            got.at[pl.ds(pl.multiple_of(group * 256 + i * 16, 16), 16)],
            ss.at[sem], rs.at[sem], device_id=device(*d), device_id_type=MESH,
        ).start()

    def back_unit(group, i, sem):
        d = (-(i // 4), -GROUPS[group], -lax.rem(i, 4))
        pltpu.make_async_remote_copy(
            ret.at[pl.ds(pl.multiple_of(group * 256 + i * 16, 16), 16)],
            back.at[pl.ds(pl.multiple_of(me * 16, 16), 16)],
            ss.at[sem], rs.at[sem], device_id=device(*d), device_id_type=MESH,
        ).start()

    def all_units(unit, chunk, sem):
        def step(j, carry):
            i = 15 - j
            unit(2 * chunk + 1, i, sem)
            if chunk == 0:
                unit(0, i, sem)
            else:

                @pl.when(i > 0)
                def _():
                    unit(2, i, sem)

            return carry

        lax.fori_loop(0, 16, step, 0)

    def landed(chunk, ref, sem):
        whole = ref.at[pl.ds(0, (32 - chunk) * 16)]
        pltpu.make_async_copy(whole, whole, sem).wait()

    all_units(out_unit, 0, 0)
    all_units(out_unit, 1, 1)
    own = pl.ds(pl.multiple_of(me * 16, 16), 16)
    own_out = pltpu.make_async_copy(send.at[own], got.at[pl.ds(512, 16)], lsem.at[0])
    own_out.start()
    own_back = pltpu.make_async_copy(ret.at[pl.ds(512, 16)], back.at[own], lsem.at[1])

    def to_other(src, dst, sem):
        return pltpu.make_async_remote_copy(
            src, dst, ps.at[sem], pr.at[sem], device_id=other, device_id_type=MESH
        )

    def unpack(src, chunk, first):
        for g in range(2):
            at = chunk * 512 + g * 256
            got_rows = dot(perm[...], src[at : at + 256, :]).astype(BF)
            to = slice(first + g * 32, first + g * 32 + 32)
            for q in range(4):
                quarter = slice(q * 512, (q + 1) * 512)
                xt[to, quarter] = got_rows[q * 64 : q * 64 + 32, :]
                xc[to, quarter] = got_rows[q * 64 + 32 : q * 64 + 64, :]

    for chunk in range(2):
        half = pl.ds(chunk * 512, 512)
        landed(chunk, got, rs.at[chunk])
        if chunk == 1:
            own_out.wait()
        share = to_other(got.at[half], got_other.at[half], chunk)
        share.start()
        unpack(got, chunk, chunk * 128)
        share.wait_recv()
        unpack(got_other, chunk, chunk * 128 + 64)
        if chunk == 0:
            for load in loads[4:]:
                load.wait()

        here = slice(chunk * 128, chunk * 128 + 128)
        gate_up = dot(xt[here, :], wgu[...])
        gate, up = gate_up[:, :384], gate_up[:, 384:]
        act_cot = dot_nt(xc[here, :], wd[...])
        sig = jax.nn.sigmoid(gate)
        act[here, :] = (gate * sig * up).astype(BF)
        gu[here, :384] = (act_cot * up * sig * (1.0 + gate * (1.0 - sig))).astype(BF)
        gu[here, 384:] = (act_cot * gate * sig).astype(BF)

        gives = []
        for q in range(4):
            quarter = slice(q * 512, (q + 1) * 512)
            cot_q = dot_nt(gu[here, :], wgu[quarter, :])
            out_q = dot(act[here, :], wd[:, quarter])
            for g in range(2):
                for a, value in enumerate((cot_q, out_q)):
                    to = q * 128 + g * 64 + a * 32
                    mine[to : to + 32, :] = value[g * 32 : g * 32 + 32, :]
                    theirs[chunk * 512 + to : chunk * 512 + to + 32, :] = value[
                        64 + g * 32 : 96 + g * 32, :
                    ].astype(BF)
            piece = pl.ds(chunk * 512 + q * 128, 128)
            give = to_other(theirs.at[piece], given.at[piece], 2 + chunk)
            give.start()
            gives.append(give)
        whole = given.at[half]
        pltpu.make_async_copy(whole, whole, pr.at[2 + chunk]).wait()

        summed[...] = (mine[...] + given[chunk * 512 : chunk * 512 + 512, :].astype(F32)).astype(BF)
        for g in range(2):
            rows_g = jnp.concatenate(
                [summed[q * 128 + g * 64 : q * 128 + g * 64 + 64, :] for q in range(4)], axis=0
            )
            at = chunk * 512 + g * 256
            ret[at : at + 256, :] = dot(perm_t[...], rows_g).astype(BF)
        all_units(back_unit, chunk, 2 + chunk)
        if chunk == 1:
            own_back.start()

    def in_grads(i, carry):
        at = pl.ds(pl.multiple_of(i * 256, 256), 256)
        both = dot_tn(xt[:, at], gu[...])
        g_gate[at, :] = both[:, :384].astype(BF)
        g_up[at, :] = both[:, 384:].astype(BF)
        return carry

    lax.fori_loop(0, 8, in_grads, 0)

    def down_grads(i, carry):
        at = pl.ds(pl.multiple_of(i * 512, 512), 512)
        g_down[:, at] = dot_tn(act[...], xc[:, at]).astype(BF)
        return carry

    lax.fori_loop(0, 4, down_grads, 0)

    for chunk in range(2):
        landed(chunk, back, rs.at[2 + chunk])
        landed(chunk, send, ss.at[chunk])
        landed(chunk, ret, ss.at[2 + chunk])
        half = pl.ds(chunk * 512, 512)
        for ref, sem in ((got, ps.at[chunk]), (theirs, ps.at[2 + chunk])):
            pltpu.make_async_copy(ref.at[half], ref.at[half], sem).wait()
    own_back.wait()


def combine(back, sel_t, g_gate, g_up, g_down, mixed, token_grad, o_gate, o_up, o_down, sems):
    stores = [
        pltpu.make_async_copy(g_gate, o_gate.at[0], sems.at[0]),
        pltpu.make_async_copy(g_up, o_up.at[0], sems.at[1]),
        pltpu.make_async_copy(g_down, o_down.at[0], sems.at[2]),
    ]
    for store in stores:
        store.start()
    both = dot(sel_t[...], back[...])
    for q in range(4):
        quarter = slice(q * 512, (q + 1) * 512)
        at = q * 64
        token_grad[:, quarter] = both[at : at + 16, :].astype(BF)
        mixed[:, quarter] = (
            both[at + 16 : at + 32, :] + both[at + 32 : at + 48, :] + both[at + 48 : at + 64, :]
        ).astype(BF)
    for store in stores:
        store.wait()


def body(tokens, route, probs, cotangent, gate_weight, up_weight, down_weight):
    any_spec = pl.BlockSpec(memory_space=pl.ANY)
    vmem_spec = pl.BlockSpec(memory_space=pltpu.VMEM)
    kept = pl.pallas_call(
        exchange,
        name="exchange",
        out_shape=[
            pltpu.VMEM((1024, 512), BF),
            pltpu.VMEM((256, 1024), BF),
            pltpu.VMEM((2048, 384), BF),
            pltpu.VMEM((2048, 384), BF),
            pltpu.VMEM((384, 2048), BF),
        ],
        in_specs=[any_spec] * 7,
        out_specs=[vmem_spec] * 5,
        scratch_shapes=[
            pltpu.VMEM((16, 8), jnp.int32),
            pltpu.VMEM((16, 8), F32),
            pltpu.VMEM((16, 2048), BF),
            pltpu.VMEM((16, 2048), BF),
            pltpu.VMEM((2048, 768), BF),
            pltpu.VMEM((384, 2048), BF),
            pltpu.VMEM((256, 256), BF),
            pltpu.VMEM((256, 256), BF),
            pltpu.VMEM((1024, 256), BF),
            pltpu.VMEM((256, 512), BF),
            pltpu.VMEM((1024, 512), BF),
            pltpu.VMEM((1024, 512), BF),
            pltpu.VMEM((1024, 512), BF),
            pltpu.VMEM((256, 2048), BF),
            pltpu.VMEM((256, 2048), BF),
            pltpu.VMEM((256, 384), BF),
            pltpu.VMEM((256, 768), BF),
            pltpu.VMEM((512, 512), F32),
            pltpu.VMEM((1024, 512), BF),
            pltpu.VMEM((1024, 512), BF),
            pltpu.VMEM((512, 512), BF),
            pltpu.VMEM((1024, 512), BF),
            pltpu.SemaphoreType.DMA((7,)),
            pltpu.SemaphoreType.DMA((4,)),
            pltpu.SemaphoreType.DMA((4,)),
            pltpu.SemaphoreType.DMA((2,)),
            pltpu.SemaphoreType.DMA((4,)),
            pltpu.SemaphoreType.DMA((4,)),
        ],
        compiler_params=pltpu.CompilerParams(
            collective_id=0, has_side_effects=True, vmem_limit_bytes=40 << 20
        ),
    )(route, probs, tokens, cotangent, gate_weight, up_weight, down_weight)
    return pl.pallas_call(
        combine,
        name="combine",
        out_shape=[
            jax.ShapeDtypeStruct(tokens.shape, BF),
            jax.ShapeDtypeStruct(tokens.shape, BF),
            jax.ShapeDtypeStruct(gate_weight.shape, BF),
            jax.ShapeDtypeStruct(up_weight.shape, BF),
            jax.ShapeDtypeStruct(down_weight.shape, BF),
        ],
        in_specs=[vmem_spec] * 5,
        out_specs=[vmem_spec] * 2 + [any_spec] * 3,
        scratch_shapes=[pltpu.SemaphoreType.DMA((3,))],
        compiler_params=pltpu.CompilerParams(vmem_limit_bytes=16 << 20),
    )(*kept)


def solution(mesh):
    rows = P(("dp", "expert"), None)
    slices = P(("dp", "expert"), None, None)
    return jax.shard_map(
        body,
        mesh=mesh,
        in_specs=(rows, rows, rows, rows, slices, slices, slices),
        out_specs=(rows, rows, slices, slices, slices),
        check_vma=False,
    )
```

```python
import functools

import jax
import jax.numpy as jnp
from jax import lax
from jax.experimental import pallas as pl
from jax.experimental.pallas import tpu as pltpu
from jax.sharding import PartitionSpec as P


BF = jnp.bfloat16
F32 = jnp.float32
MESH = pl.DeviceIdType.MESH
CHUNKS = ((0, 1), (2, 3))


def dot(a, b):
    return jnp.dot(a, b, preferred_element_type=F32)


def dot_nt(a, b):
    return lax.dot_general(a, b, (((1,), (1,)), ((), ())), preferred_element_type=F32)


def dot_tn(a, b):
    return lax.dot_general(a, b, (((0,), (0,)), ((), ())), preferred_element_type=F32)


def iota(shape, dim):
    return lax.broadcasted_iota(jnp.int32, shape, dim)


def exchange(
    route_h, probs_h, tok_h, cot_h, wg_h, wu_h, wd_h,
    back, sel_t, g_gate, g_up, g_down,
    route_v, probs_v, tok_v, cot_v, wgu, wd, wgu_t, wd_t, perm, perm_t, sel, parts, send, got,
    got_other, xt, xc, act, gu, mine, theirs, given, ret,
    hsem, ss, rs, lsem, ps, pr,
):
    dp, ex = lax.axis_index("dp"), lax.axis_index("expert")
    x, y, z, c = lax.rem(dp, 4), dp // 4, ex // 2, lax.rem(ex, 2)

    xs = [lax.rem(x + d, 4) for d in range(4)]
    ys = [lax.rem(y + d, 4) for d in range(4)]
    zs = [lax.rem(z + d, 4) for d in range(4)]
    x4s, y4s = [v * 4 for v in xs], [v * 4 for v in ys]
    z2s = [v * 2 + c for v in zs]
    x64s, y256s, z16s = [v * 64 for v in xs], [v * 256 for v in ys], [v * 16 for v in zs]

    def device(dx, dy, dz):
        return (y4s[dy % 4] + xs[dx % 4], z2s[dz % 4])

    def chip_rows(dx, dy, dz):
        row = y256s[dy % 4] + x64s[dx % 4] + z16s[dz % 4]
        return pl.ds(pl.multiple_of(row, 16), 16)

    other = (dp, z * 2 + 1 - c)
    own = chip_rows(0, 0, 0)

    barrier = pltpu.get_barrier_semaphore()

    far = sorted(
        ((dx, dy, dz) for dx in range(4) for dy in range(4) for dz in range(4)),
        key=lambda d: -sum(min(v, 4 - v) for v in d),
    )
    for d in far[:63]:
        pl.semaphore_signal(barrier, 1, device_id=device(*d), device_id_type=MESH)
    pl.semaphore_signal(barrier, 1, device_id=other, device_id_type=MESH)

    loads = [
        pltpu.make_async_copy(route_h, route_v, hsem.at[0]),
        pltpu.make_async_copy(probs_h, probs_v, hsem.at[1]),
        pltpu.make_async_copy(tok_h, tok_v, hsem.at[2]),
        pltpu.make_async_copy(cot_h, cot_v, hsem.at[3]),
        pltpu.make_async_copy(wg_h.at[0], wgu.at[:, pl.ds(0, 384)], hsem.at[4]),
        pltpu.make_async_copy(wu_h.at[0], wgu.at[:, pl.ds(384, 384)], hsem.at[5]),
        pltpu.make_async_copy(wd_h.at[0], wd, hsem.at[6]),
    ]
    for load in loads:
        load.start()

    def where_from(o):
        return (o // 2 % 16) * 16 + (o // 64) * 4 + (o // 32 % 2) * 2 + o % 2

    rows, cols = iota((256, 256), 0), iota((256, 256), 1)
    perm[...] = jnp.where(cols == where_from(rows), 1.0, 0.0).astype(BF)
    perm_t[...] = jnp.where(rows == where_from(cols), 1.0, 0.0).astype(BF)

    loads[0].wait()
    loads[1].wait()
    route, probs = route_v[...].T, probs_v[...].T
    lane = iota((16, 128), 1)
    hits = jnp.zeros((16, 128), F32)
    weights = jnp.zeros((16, 128), F32)
    for k in range(8):
        same = route[:, k : k + 1] == lane % 64
        hits = hits + jnp.where(same, 1.0, 0.0)
        weights = weights + jnp.where(same, probs[:, k : k + 1], 0.0)
    earlier = jnp.where(iota((16, 16), 1) < iota((16, 16), 0), 1.0, 0.0).astype(BF)
    before = dot(earlier, hits.astype(BF)).astype(jnp.int32)
    slot = jnp.where(before == lane // 64, hits, 0.0)
    weights = weights * slot
    high = weights.astype(BF)
    rest = weights - high.astype(F32)
    middle = rest.astype(BF)
    low = (rest - middle.astype(F32)).astype(BF)
    spread = jnp.concatenate([slot.astype(BF), high, middle, low] * 4, axis=0)

    loads[2].wait()
    loads[3].wait()
    for q in range(4):
        quarter = slice(q * 512, (q + 1) * 512)
        parts[q * 64 : q * 64 + 16, :] = tok_v[:, quarter]
        for a in range(1, 4):
            parts[q * 64 + a * 16 : q * 64 + a * 16 + 16, :] = cot_v[:, quarter]

    for block in range(4):
        row = iota((256, 128), 0) + block * 256
        lane = iota((256, 128), 1)
        place = (row // 16 == lane % 64) & (row % 2 == lane // 64)
        picked = dot_nt(jnp.where(place, 1.0, 0.0).astype(BF), spread)
        row, col = iota((256, 256), 0), iota((256, 256), 1)
        right = (row // 4 % 4 == col // 64) & (
            (row // 2 % 2 == 1) == (col // 16 % 4 != 0)
        )
        picked = jnp.where(right, picked, 0.0)
        here = slice(block * 256, (block + 1) * 256)
        sel[here, :] = picked.astype(BF)
        send[here, :] = dot(sel[here, :], parts[...]).astype(BF)
        sel_t[:, here] = picked.T.astype(BF)

    pl.semaphore_wait(barrier, 64)

    def displacement(group, i):
        dx, dz = i // 4, i % 4
        return dx, (group - dx - dz) % 4, dz

    def out_unit(group, i):
        d = displacement(group, i)
        pltpu.make_async_remote_copy(
            send.at[chip_rows(*d)],
            got.at[pl.ds(group * 256 + i * 16, 16)],
            ss.at[group], rs.at[group], device_id=device(*d), device_id_type=MESH,
        ).start()

    def back_unit(group, i):
        dx, dy, dz = displacement(group, i)
        pltpu.make_async_remote_copy(
            ret.at[pl.ds(group * 256 + i * 16, 16)],
            back.at[own],
            ss.at[4 + group], rs.at[4 + group],
            device_id=device(-dx, -dy, -dz), device_id_type=MESH,
        ).start()

    def all_units(unit, group):
        for i in reversed(range(16)):
            if group or i:
                unit(group, i)

    def landed(group, ref, sem):
        whole = ref.at[pl.ds(0, 256 if group else 240)]
        pltpu.make_async_copy(whole, whole, sem).wait()

    for group in range(4):
        all_units(out_unit, group)
    own_out = pltpu.make_async_copy(send.at[own], got.at[pl.ds(0, 16)], lsem.at[0])
    own_out.start()
    own_back = pltpu.make_async_copy(ret.at[pl.ds(0, 16)], back.at[own], lsem.at[1])

    for load in loads[4:]:
        load.wait()

    def transpose(i, carry):
        at = pl.ds(pl.multiple_of(i * 256, 256), 256)
        wgu_t[:, at] = wgu[at, :].T
        wd_t[at, :] = wd[:, at].T
        return carry

    lax.fori_loop(0, 8, transpose, 0)

    def to_other(src, dst, sem):
        return pltpu.make_async_remote_copy(
            src, dst, ps.at[sem], pr.at[sem], device_id=other, device_id_type=MESH
        )

    def unpack(src, group, first):
        at = group * 256
        got_rows = dot(perm[...], src[at : at + 256, :]).astype(BF)
        to = slice(first, first + 32)
        for q in range(4):
            quarter = slice(q * 512, (q + 1) * 512)
            xt[to, quarter] = got_rows[q * 64 : q * 64 + 32, :]
            xc[to, quarter] = got_rows[q * 64 + 32 : q * 64 + 64, :]

    def share(group):
        at = pl.ds(group * 256, 256)
        return to_other(got.at[at], got_other.at[at], group)

    def arrive(chunk):
        groups = CHUNKS[chunk]
        first = groups[0] * 64
        for group in groups:
            landed(group, got, rs.at[group])
            if group == 0:
                own_out.wait()
            share(group).start()
        for n, group in enumerate(groups):
            unpack(got, group, first + n * 32)

    def work(chunk):
        groups = CHUNKS[chunk]
        count = len(groups)
        first, half = groups[0] * 64, count * 32
        for n, group in enumerate(groups):
            share(group).wait_recv()
            unpack(got_other, group, first + half + n * 32)
        here = slice(first, first + 2 * half)
        gate_up = dot(xt[here, :], wgu[...])
        gate, up = gate_up[:, :384], gate_up[:, 384:]
        act_cot = dot(xc[here, :], wd_t[...])
        sig = jax.nn.sigmoid(gate)
        act[here, :] = (gate * sig * up).astype(BF)
        gu[here, :384] = (act_cot * up * sig * (1.0 + gate * (1.0 - sig))).astype(BF)
        gu[here, 384:] = (act_cot * gate * sig).astype(BF)
        base, size = groups[0] * 256, count * 64
        for pair in range(2):
            columns = slice(pair * 1024, (pair + 1) * 1024)
            cot_half = dot(gu[here, :], wgu_t[:, columns])
            out_half = dot(act[here, :], wd[:, columns])
            for q in (pair * 2, pair * 2 + 1):
                quarter = slice((q % 2) * 512, (q % 2) * 512 + 512)
                for n in range(count):
                    for a, value in enumerate((cot_half[:, quarter], out_half[:, quarter])):
                        to = base + q * size + n * 64 + a * 32
                        at = n * 32
                        mine[to : to + 32, :] = value[at : at + 32, :]
                        theirs[to : to + 32, :] = value[half + at : half + at + 32, :].astype(BF)
            piece = pl.ds(base + pair * 2 * size, 2 * size)
            to_other(theirs.at[piece], given.at[piece], 4 + chunk).start()

    def finish(chunk):
        groups = CHUNKS[chunk]
        count = len(groups)
        base, size = groups[0] * 256, count * 64
        whole = given.at[pl.ds(base, count * 256)]
        pltpu.make_async_copy(whole, whole, pr.at[4 + chunk]).wait()
        for n, group in enumerate(groups):
            pieces = []
            for q in range(4):
                at = base + q * size + n * 64
                pieces.append(
                    (mine[at : at + 64, :] + given[at : at + 64, :].astype(F32)).astype(BF)
                )
            back_rows = dot(perm_t[...], jnp.concatenate(pieces, axis=0)).astype(BF)
            ret[group * 256 : group * 256 + 256, :] = back_rows
        for group in groups:
            all_units(back_unit, group)
            if group == 0:
                own_back.start()

    def in_grads(i, carry):
        at = pl.ds(pl.multiple_of(i * 256, 256), 256)
        both = dot_tn(xt[:, at], gu[...])
        g_gate[at, :] = both[:, :384].astype(BF)
        g_up[at, :] = both[:, 384:].astype(BF)
        return carry

    def down_grads(i, carry):
        at = pl.ds(pl.multiple_of(i * 512, 512), 512)
        g_down[:, at] = dot_tn(act[...], xc[:, at]).astype(BF)
        return carry

    for chunk in range(len(CHUNKS)):
        arrive(chunk)
        if chunk:
            finish(chunk - 1)
        work(chunk)
    lax.fori_loop(0, 4, down_grads, 0)
    finish(len(CHUNKS) - 1)
    lax.fori_loop(0, 8, in_grads, 0)

    for group in range(4):
        landed(group, back, rs.at[4 + group])
        landed(group, send, ss.at[group])
        landed(group, ret, ss.at[4 + group])
        share(group).wait_send()
    for chunk, groups in enumerate(CHUNKS):
        whole = theirs.at[pl.ds(0, len(groups) * 256)]
        pltpu.make_async_copy(whole, whole, ps.at[4 + chunk]).wait()
    own_back.wait()


def combine(
    back, sel_t, g_gate, g_up, g_down,
    o_mixed, o_token, o_gate, o_up, o_down, mixed, token_grad, sems,
):
    stores = [
        pltpu.make_async_copy(src, dst, sems.at[n])
        for n, (src, dst) in enumerate((
            (g_gate, o_gate.at[0]), (g_up, o_up.at[0]), (g_down, o_down.at[0]),
            (mixed, o_mixed), (token_grad, o_token),
        ))
    ]
    for store in stores[:3]:
        store.start()
    both = dot(sel_t[...], back[...])
    for q in range(4):
        quarter = slice(q * 512, (q + 1) * 512)
        at = q * 64
        token_grad[:, quarter] = both[at : at + 16, :].astype(BF)
        mixed[:, quarter] = (
            both[at + 16 : at + 32, :] + both[at + 32 : at + 48, :] + both[at + 48 : at + 64, :]
        ).astype(BF)
    for store in stores[3:]:
        store.start()
    for store in stores:
        store.wait()


def body(tokens, route, probs, cotangent, gate_weight, up_weight, down_weight):
    hbm_spec = pl.BlockSpec(memory_space=pltpu.HBM)
    vmem_spec = pl.BlockSpec(memory_space=pltpu.VMEM)
    kept = pl.pallas_call(
        exchange,
        name="exchange",
        out_shape=[
            pltpu.VMEM((1024, 512), BF),
            pltpu.VMEM((256, 1024), BF),
            pltpu.VMEM((2048, 384), BF),
            pltpu.VMEM((2048, 384), BF),
            pltpu.VMEM((384, 2048), BF),
        ],
        in_specs=[hbm_spec] * 7,
        out_specs=[vmem_spec] * 5,
        scratch_shapes=[
            pltpu.VMEM((8, 16), jnp.int32),
            pltpu.VMEM((8, 16), F32),
            pltpu.VMEM((16, 2048), BF),
            pltpu.VMEM((16, 2048), BF),
            pltpu.VMEM((2048, 768), BF),
            pltpu.VMEM((384, 2048), BF),
            pltpu.VMEM((768, 2048), BF),
            pltpu.VMEM((2048, 384), BF),
            pltpu.VMEM((256, 256), BF),
            pltpu.VMEM((256, 256), BF),
            pltpu.VMEM((1024, 256), BF),
            pltpu.VMEM((256, 512), BF),
            pltpu.VMEM((1024, 512), BF),
            pltpu.VMEM((1024, 512), BF),
            pltpu.VMEM((1024, 512), BF),
            pltpu.VMEM((256, 2048), BF),
            pltpu.VMEM((256, 2048), BF),
            pltpu.VMEM((256, 384), BF),
            pltpu.VMEM((256, 768), BF),
            pltpu.VMEM((1024, 512), F32),
            pltpu.VMEM((1024, 512), BF),
            pltpu.VMEM((1024, 512), BF),
            pltpu.VMEM((1024, 512), BF),
            pltpu.SemaphoreType.DMA((7,)),
            pltpu.SemaphoreType.DMA((8,)),
            pltpu.SemaphoreType.DMA((8,)),
            pltpu.SemaphoreType.DMA((2,)),
            pltpu.SemaphoreType.DMA((8,)),
            pltpu.SemaphoreType.DMA((8,)),
        ],
        compiler_params=pltpu.CompilerParams(
            collective_id=0, has_side_effects=True, vmem_limit_bytes=60751872
        ),
    )(route.T, probs.T, tokens, cotangent, gate_weight, up_weight, down_weight)
    return pl.pallas_call(
        combine,
        name="combine",
        out_shape=[
            jax.ShapeDtypeStruct(tokens.shape, BF),
            jax.ShapeDtypeStruct(tokens.shape, BF),
            jax.ShapeDtypeStruct(gate_weight.shape, BF),
            jax.ShapeDtypeStruct(up_weight.shape, BF),
            jax.ShapeDtypeStruct(down_weight.shape, BF),
        ],
        in_specs=[vmem_spec] * 5,
        out_specs=[hbm_spec] * 5,
        scratch_shapes=[
            pltpu.VMEM(tokens.shape, BF),
            pltpu.VMEM(tokens.shape, BF),
            pltpu.SemaphoreType.DMA((5,)),
        ],
        compiler_params=pltpu.CompilerParams(vmem_limit_bytes=16 << 20),
    )(*kept)


def solution(mesh):
    rows = P(("dp", "expert"), None)
    slices = P(("dp", "expert"), None, None)
    return jax.shard_map(
        body,
        mesh=mesh,
        in_specs=(rows, rows, rows, rows, slices, slices, slices),
        out_specs=(rows, rows, slices, slices, slices),
        check_vma=False,
    )
```

```python
import functools

import jax
import jax.numpy as jnp
from jax import lax
from jax.experimental import pallas as pl
from jax.experimental.pallas import tpu as pltpu
from jax.sharding import PartitionSpec as P


BF = jnp.bfloat16
F32 = jnp.float32
MESH = pl.DeviceIdType.MESH
TURN = (0, 1, 2, 3)


def hops(d):
    return sum(min(v, 4 - v) for v in d)


ORDER = sorted(
    ((dx, dy, dz) for dx in range(4) for dy in range(4) for dz in range(4)),
    key=lambda d: (TURN.index(sum(d) % 4), -hops(d), d),
)
HOME = ORDER.index((0, 0, 0))
CHUNKS = ((0,), (1,), (2,), (3,))


def dot(a, b):
    return jnp.dot(a, b, preferred_element_type=F32)


def dot_nt(a, b):
    return lax.dot_general(a, b, (((1,), (1,)), ((), ())), preferred_element_type=F32)


def dot_tn(a, b):
    return lax.dot_general(a, b, (((0,), (0,)), ((), ())), preferred_element_type=F32)


def iota(shape, dim):
    return lax.broadcasted_iota(jnp.int32, shape, dim)


def exchange(
    route_h, probs_h, tok_h, cot_h, wg_h, wu_h, wd_h,
    back, sel_t, g_gate, g_up, g_down,
    route_v, probs_v, tok_v, cot_v, wgu, wd, wgu_t, wd_t, perm, perm_t, sel, parts, send, got,
    got_other, xt, xc, act, gu, mine, theirs, given, ret,
    hsem, ss, rs, lsem, ps, pr,
):
    dp, ex = lax.axis_index("dp"), lax.axis_index("expert")
    x, y, z, c = lax.rem(dp, 4), dp // 4, ex // 2, lax.rem(ex, 2)

    xs = [lax.rem(x + d, 4) for d in range(4)]
    ys = [lax.rem(y + d, 4) for d in range(4)]
    zs = [lax.rem(z + d, 4) for d in range(4)]
    x4s, y4s = [v * 4 for v in xs], [v * 4 for v in ys]
    z2s = [v * 2 + c for v in zs]
    x64s, y256s, z16s = [v * 64 for v in xs], [v * 256 for v in ys], [v * 16 for v in zs]

    def device(dx, dy, dz):
        return (y4s[dy % 4] + xs[dx % 4], z2s[dz % 4])

    def chip_rows(dx, dy, dz):
        row = y256s[dy % 4] + x64s[dx % 4] + z16s[dz % 4]
        return pl.ds(pl.multiple_of(row, 16), 16)

    other = (dp, z * 2 + 1 - c)
    own = chip_rows(0, 0, 0)

    barrier = pltpu.get_barrier_semaphore()

    for d in sorted(ORDER, key=hops, reverse=True)[:63]:
        pl.semaphore_signal(barrier, 1, device_id=device(*d), device_id_type=MESH)
    pl.semaphore_signal(barrier, 1, device_id=other, device_id_type=MESH)

    loads = [
        pltpu.make_async_copy(route_h, route_v, hsem.at[0]),
        pltpu.make_async_copy(probs_h, probs_v, hsem.at[1]),
        pltpu.make_async_copy(tok_h, tok_v, hsem.at[2]),
        pltpu.make_async_copy(cot_h, cot_v, hsem.at[3]),
        pltpu.make_async_copy(wg_h.at[0], wgu.at[:, pl.ds(0, 384)], hsem.at[4]),
        pltpu.make_async_copy(wu_h.at[0], wgu.at[:, pl.ds(384, 384)], hsem.at[5]),
        pltpu.make_async_copy(wd_h.at[0], wd, hsem.at[6]),
    ]
    for load in loads:
        load.start()

    def where_from(o):
        return (o // 2 % 16) * 16 + (o // 64) * 4 + (o // 32 % 2) * 2 + o % 2

    rows, cols = iota((256, 256), 0), iota((256, 256), 1)
    perm[...] = jnp.where(cols == where_from(rows), 1.0, 0.0).astype(BF)
    perm_t[...] = jnp.where(rows == where_from(cols), 1.0, 0.0).astype(BF)

    loads[0].wait()
    loads[1].wait()
    route, probs = route_v[...].T, probs_v[...].T
    lane = iota((16, 128), 1)
    hits = jnp.zeros((16, 128), F32)
    weights = jnp.zeros((16, 128), F32)
    for k in range(8):
        same = route[:, k : k + 1] == lane % 64
        hits = hits + jnp.where(same, 1.0, 0.0)
        weights = weights + jnp.where(same, probs[:, k : k + 1], 0.0)
    earlier = jnp.where(iota((16, 16), 1) < iota((16, 16), 0), 1.0, 0.0).astype(BF)
    before = dot(earlier, hits.astype(BF)).astype(jnp.int32)
    slot = jnp.where(before == lane // 64, hits, 0.0)
    weights = weights * slot
    high = weights.astype(BF)
    rest = weights - high.astype(F32)
    middle = rest.astype(BF)
    low = (rest - middle.astype(F32)).astype(BF)
    spread = jnp.concatenate([slot.astype(BF), high, middle, low] * 4, axis=0)

    loads[2].wait()
    loads[3].wait()
    for q in range(4):
        quarter = slice(q * 512, (q + 1) * 512)
        parts[q * 64 : q * 64 + 16, :] = tok_v[:, quarter]
        for a in range(1, 4):
            parts[q * 64 + a * 16 : q * 64 + a * 16 + 16, :] = cot_v[:, quarter]

    for block in range(4):
        row = iota((256, 128), 0) + block * 256
        lane = iota((256, 128), 1)
        place = (row // 16 == lane % 64) & (row % 2 == lane // 64)
        picked = dot_nt(jnp.where(place, 1.0, 0.0).astype(BF), spread)
        row, col = iota((256, 256), 0), iota((256, 256), 1)
        right = (row // 4 % 4 == col // 64) & (
            (row // 2 % 2 == 1) == (col // 16 % 4 != 0)
        )
        picked = jnp.where(right, picked, 0.0)
        here = slice(block * 256, (block + 1) * 256)
        sel[here, :] = picked.astype(BF)
        send[here, :] = dot(sel[here, :], parts[...]).astype(BF)
        sel_t[:, here] = picked.T.astype(BF)

    pl.semaphore_wait(barrier, 64)

    def out_unit(group, i):
        d = ORDER[group * 16 + i]
        pltpu.make_async_remote_copy(
            send.at[chip_rows(*d)],
            got.at[pl.ds(group * 256 + i * 16, 16)],
            ss.at[group], rs.at[group], device_id=device(*d), device_id_type=MESH,
        ).start()

    def back_unit(group, i):
        dx, dy, dz = ORDER[group * 16 + i]
        pltpu.make_async_remote_copy(
            ret.at[pl.ds(group * 256 + i * 16, 16)],
            back.at[own],
            ss.at[4 + group], rs.at[4 + group],
            device_id=device(-dx, -dy, -dz), device_id_type=MESH,
        ).start()

    def all_units(unit, group):
        for i in range(16):
            if group * 16 + i != HOME:
                unit(group, i)

    def landed(group, ref, sem):
        whole = ref.at[pl.ds(0, 240 if group == HOME // 16 else 256)]
        pltpu.make_async_copy(whole, whole, sem).wait()

    for group in range(4):
        all_units(out_unit, group)
    own_out = pltpu.make_async_copy(send.at[own], got.at[pl.ds(HOME * 16, 16)], lsem.at[0])
    own_out.start()
    own_back = pltpu.make_async_copy(ret.at[pl.ds(HOME * 16, 16)], back.at[own], lsem.at[1])

    for load in loads[4:]:
        load.wait()

    def transpose(i, carry):
        at = pl.ds(pl.multiple_of(i * 256, 256), 256)
        wgu_t[:, at] = wgu[at, :].T
        wd_t[at, :] = wd[:, at].T
        return carry

    lax.fori_loop(0, 8, transpose, 0)

    def to_other(src, dst, sem):
        return pltpu.make_async_remote_copy(
            src, dst, ps.at[sem], pr.at[sem], device_id=other, device_id_type=MESH
        )

    def unpack(src, group, first):
        at = group * 256
        got_rows = dot(perm[...], src[at : at + 256, :]).astype(BF)
        to = slice(first, first + 32)
        for q in range(4):
            quarter = slice(q * 512, (q + 1) * 512)
            xt[to, quarter] = got_rows[q * 64 : q * 64 + 32, :]
            xc[to, quarter] = got_rows[q * 64 + 32 : q * 64 + 64, :]

    def share(group):
        at = pl.ds(group * 256, 256)
        return to_other(got.at[at], got_other.at[at], group)

    def arrive(chunk):
        groups = CHUNKS[chunk]
        for group in groups:
            landed(group, got, rs.at[group])
            if group == HOME // 16:
                own_out.wait()
            share(group).start()

    def open_own(chunk):
        groups = CHUNKS[chunk]
        for n, group in enumerate(groups):
            unpack(got, group, groups[0] * 64 + n * 32)

    def first_half(chunk):
        groups = CHUNKS[chunk]
        count = len(groups)
        first, half = groups[0] * 64, count * 32
        for n, group in enumerate(groups):
            share(group).wait_recv()
            unpack(got_other, group, first + half + n * 32)
        here = slice(first, first + 2 * half)
        gate_up = dot(xt[here, :], wgu[...])
        gate, up = gate_up[:, :384], gate_up[:, 384:]
        act_cot = dot(xc[here, :], wd_t[...])
        sig = jax.nn.sigmoid(gate)
        act[here, :] = (gate * sig * up).astype(BF)
        gu[here, :384] = (act_cot * up * sig * (1.0 + gate * (1.0 - sig))).astype(BF)
        gu[here, 384:] = (act_cot * gate * sig).astype(BF)

    def second_half(chunk):
        groups = CHUNKS[chunk]
        count = len(groups)
        first, half = groups[0] * 64, count * 32
        here = slice(first, first + 2 * half)
        base, size = groups[0] * 256, count * 64
        for pair in range(2):
            columns = slice(pair * 1024, (pair + 1) * 1024)
            cot_half = dot(gu[here, :], wgu_t[:, columns])
            out_half = dot(act[here, :], wd[:, columns])
            for q in (pair * 2, pair * 2 + 1):
                quarter = slice((q % 2) * 512, (q % 2) * 512 + 512)
                for n in range(count):
                    for a, value in enumerate((cot_half[:, quarter], out_half[:, quarter])):
                        to = base + q * size + n * 64 + a * 32
                        at = n * 32
                        mine[to : to + 32, :] = value[at : at + 32, :]
                        theirs[to : to + 32, :] = value[half + at : half + at + 32, :].astype(BF)
            piece = pl.ds(base + pair * 2 * size, 2 * size)
            to_other(theirs.at[piece], given.at[piece], 4 + chunk).start()

    def finish(chunk):
        groups = CHUNKS[chunk]
        count = len(groups)
        base, size = groups[0] * 256, count * 64
        whole = given.at[pl.ds(base, count * 256)]
        pltpu.make_async_copy(whole, whole, pr.at[4 + chunk]).wait()
        for n, group in enumerate(groups):
            pieces = []
            for q in range(4):
                at = base + q * size + n * 64
                pieces.append(
                    (mine[at : at + 64, :] + given[at : at + 64, :].astype(F32)).astype(BF)
                )
            back_rows = dot(perm_t[...], jnp.concatenate(pieces, axis=0)).astype(BF)
            ret[group * 256 : group * 256 + 256, :] = back_rows
        for group in groups:
            all_units(back_unit, group)
            if group == HOME // 16:
                own_back.start()

    def in_grads(i, carry):
        at = pl.ds(pl.multiple_of(i * 256, 256), 256)
        both = dot_tn(xt[:, at], gu[...])
        g_gate[at, :] = both[:, :384].astype(BF)
        g_up[at, :] = both[:, 384:].astype(BF)
        return carry

    def down_grads(i, carry):
        at = pl.ds(pl.multiple_of(i * 512, 512), 512)
        g_down[:, at] = dot_tn(act[...], xc[:, at]).astype(BF)
        return carry

    arrive(0)
    open_own(0)
    for chunk in range(len(CHUNKS)):
        first_half(chunk)
        if chunk:
            finish(chunk - 1)
        if chunk + 1 < len(CHUNKS):
            arrive(chunk + 1)
        second_half(chunk)
        if chunk + 1 < len(CHUNKS):
            open_own(chunk + 1)
    lax.fori_loop(0, 4, down_grads, 0)
    finish(len(CHUNKS) - 1)
    lax.fori_loop(0, 8, in_grads, 0)

    for group in range(4):
        landed(group, back, rs.at[4 + group])
        landed(group, send, ss.at[group])
        landed(group, ret, ss.at[4 + group])
        share(group).wait_send()
    for chunk, groups in enumerate(CHUNKS):
        whole = theirs.at[pl.ds(0, len(groups) * 256)]
        pltpu.make_async_copy(whole, whole, ps.at[4 + chunk]).wait()
    own_back.wait()


def combine(
    back, sel_t, g_gate, g_up, g_down,
    o_mixed, o_token, o_gate, o_up, o_down, mixed, token_grad, sems,
):
    stores = [
        pltpu.make_async_copy(src, dst, sems.at[n])
        for n, (src, dst) in enumerate((
            (g_gate, o_gate.at[0]), (g_up, o_up.at[0]), (g_down, o_down.at[0]),
            (mixed, o_mixed), (token_grad, o_token),
        ))
    ]
    for store in stores[:3]:
        store.start()
    both = dot(sel_t[...], back[...])
    for q in range(4):
        quarter = slice(q * 512, (q + 1) * 512)
        at = q * 64
        token_grad[:, quarter] = both[at : at + 16, :].astype(BF)
        mixed[:, quarter] = (
            both[at + 16 : at + 32, :] + both[at + 32 : at + 48, :] + both[at + 48 : at + 64, :]
        ).astype(BF)
    for store in stores[3:]:
        store.start()
    for store in stores:
        store.wait()


def body(tokens, route, probs, cotangent, gate_weight, up_weight, down_weight):
    hbm_spec = pl.BlockSpec(memory_space=pltpu.HBM)
    vmem_spec = pl.BlockSpec(memory_space=pltpu.VMEM)
    kept = pl.pallas_call(
        exchange,
        name="exchange",
        out_shape=[
            pltpu.VMEM((1024, 512), BF),
            pltpu.VMEM((256, 1024), BF),
            pltpu.VMEM((2048, 384), BF),
            pltpu.VMEM((2048, 384), BF),
            pltpu.VMEM((384, 2048), BF),
        ],
        in_specs=[hbm_spec] * 7,
        out_specs=[vmem_spec] * 5,
        scratch_shapes=[
            pltpu.VMEM((8, 16), jnp.int32),
            pltpu.VMEM((8, 16), F32),
            pltpu.VMEM((16, 2048), BF),
            pltpu.VMEM((16, 2048), BF),
            pltpu.VMEM((2048, 768), BF),
            pltpu.VMEM((384, 2048), BF),
            pltpu.VMEM((768, 2048), BF),
            pltpu.VMEM((2048, 384), BF),
            pltpu.VMEM((256, 256), BF),
            pltpu.VMEM((256, 256), BF),
            pltpu.VMEM((1024, 256), BF),
            pltpu.VMEM((256, 512), BF),
            pltpu.VMEM((1024, 512), BF),
            pltpu.VMEM((1024, 512), BF),
            pltpu.VMEM((1024, 512), BF),
            pltpu.VMEM((256, 2048), BF),
            pltpu.VMEM((256, 2048), BF),
            pltpu.VMEM((256, 384), BF),
            pltpu.VMEM((256, 768), BF),
            pltpu.VMEM((1024, 512), F32),
            pltpu.VMEM((1024, 512), BF),
            pltpu.VMEM((1024, 512), BF),
            pltpu.VMEM((1024, 512), BF),
            pltpu.SemaphoreType.DMA((7,)),
            pltpu.SemaphoreType.DMA((8,)),
            pltpu.SemaphoreType.DMA((8,)),
            pltpu.SemaphoreType.DMA((2,)),
            pltpu.SemaphoreType.DMA((8,)),
            pltpu.SemaphoreType.DMA((8,)),
        ],
        compiler_params=pltpu.CompilerParams(
            collective_id=0, has_side_effects=True, vmem_limit_bytes=60751872
        ),
    )(route.T, probs.T, tokens, cotangent, gate_weight, up_weight, down_weight)
    return pl.pallas_call(
        combine,
        name="combine",
        out_shape=[
            jax.ShapeDtypeStruct(tokens.shape, BF),
            jax.ShapeDtypeStruct(tokens.shape, BF),
            jax.ShapeDtypeStruct(gate_weight.shape, BF),
            jax.ShapeDtypeStruct(up_weight.shape, BF),
            jax.ShapeDtypeStruct(down_weight.shape, BF),
        ],
        in_specs=[vmem_spec] * 5,
        out_specs=[hbm_spec] * 5,
        scratch_shapes=[
            pltpu.VMEM(tokens.shape, BF),
            pltpu.VMEM(tokens.shape, BF),
            pltpu.SemaphoreType.DMA((5,)),
        ],
        compiler_params=pltpu.CompilerParams(vmem_limit_bytes=16 << 20),
    )(*kept)


def solution(mesh):
    rows = P(("dp", "expert"), None)
    slices = P(("dp", "expert"), None, None)
    return jax.shard_map(
        body,
        mesh=mesh,
        in_specs=(rows, rows, rows, rows, slices, slices, slices),
        out_specs=(rows, rows, slices, slices, slices),
        check_vma=False,
    )
```

```python
import functools

import jax
import jax.numpy as jnp
from jax import lax
from jax.experimental import pallas as pl
from jax.experimental.pallas import tpu as pltpu
from jax.sharding import PartitionSpec as P


BF = jnp.bfloat16
F32 = jnp.float32
MESH = pl.DeviceIdType.MESH
TURN = (2, 1, 3, 0)


def hops(d):
    return sum(min(v, 4 - v) for v in d)


ORDER = sorted(
    ((dx, dy, dz) for dx in range(4) for dy in range(4) for dz in range(4)),
    key=lambda d: (TURN.index(sum(d) % 4), -hops(d), d),
)
HOME = ORDER.index((0, 0, 0))
CHUNKS = ((0,), (1,), (2,), (3,))


def dot(a, b):
    return jnp.dot(a, b, preferred_element_type=F32)


def dot_nt(a, b):
    return lax.dot_general(a, b, (((1,), (1,)), ((), ())), preferred_element_type=F32)


def dot_tn(a, b):
    return lax.dot_general(a, b, (((0,), (0,)), ((), ())), preferred_element_type=F32)


def iota(shape, dim):
    return lax.broadcasted_iota(jnp.int32, shape, dim)


def exchange(
    route_h, probs_h, tok_h, cot_h, wg_h, wu_h, wd_h,
    back, sel_t, g_gate, g_up, g_down,
    route_v, probs_v, tok_v, cot_v, wgu, wd, wgu_t, wd_t, perm, perm_t, sel, parts, send, got,
    got_other, xt, xc, act, gu, mine, theirs, given, ret,
    hsem, ss, rs, lsem, ps, pr,
):
    dp, ex = lax.axis_index("dp"), lax.axis_index("expert")
    x, y, z, c = lax.rem(dp, 4), dp // 4, ex // 2, lax.rem(ex, 2)

    xs = [lax.rem(x + d, 4) for d in range(4)]
    ys = [lax.rem(y + d, 4) for d in range(4)]
    zs = [lax.rem(z + d, 4) for d in range(4)]
    x4s, y4s = [v * 4 for v in xs], [v * 4 for v in ys]
    z2s = [v * 2 + c for v in zs]
    x64s, y256s, z16s = [v * 64 for v in xs], [v * 256 for v in ys], [v * 16 for v in zs]

    def device(dx, dy, dz):
        return (y4s[dy % 4] + xs[dx % 4], z2s[dz % 4])

    def chip_rows(dx, dy, dz):
        row = y256s[dy % 4] + x64s[dx % 4] + z16s[dz % 4]
        return pl.ds(pl.multiple_of(row, 16), 16)

    other = (dp, z * 2 + 1 - c)
    own = chip_rows(0, 0, 0)

    barrier = pltpu.get_barrier_semaphore()

    for d in sorted(ORDER, key=hops, reverse=True)[:63]:
        pl.semaphore_signal(barrier, 1, device_id=device(*d), device_id_type=MESH)
    pl.semaphore_signal(barrier, 1, device_id=other, device_id_type=MESH)

    loads = [
        pltpu.make_async_copy(route_h, route_v, hsem.at[0]),
        pltpu.make_async_copy(probs_h, probs_v, hsem.at[1]),
        pltpu.make_async_copy(tok_h, tok_v, hsem.at[2]),
        pltpu.make_async_copy(cot_h, cot_v, hsem.at[3]),
        pltpu.make_async_copy(wg_h.at[0], wgu.at[:, pl.ds(0, 384)], hsem.at[4]),
        pltpu.make_async_copy(wu_h.at[0], wgu.at[:, pl.ds(384, 384)], hsem.at[5]),
        pltpu.make_async_copy(wd_h.at[0], wd, hsem.at[6]),
    ]
    for load in loads:
        load.start()

    def where_from(o):
        return (o // 2 % 16) * 16 + (o // 64) * 4 + (o // 32 % 2) * 2 + o % 2

    rows, cols = iota((256, 256), 0), iota((256, 256), 1)
    perm[...] = jnp.where(cols == where_from(rows), 1.0, 0.0).astype(BF)
    perm_t[...] = jnp.where(rows == where_from(cols), 1.0, 0.0).astype(BF)

    loads[0].wait()
    loads[1].wait()
    route, probs = route_v[...].T, probs_v[...].T
    lane = iota((16, 128), 1)
    hits = jnp.zeros((16, 128), F32)
    weights = jnp.zeros((16, 128), F32)
    for k in range(8):
        same = route[:, k : k + 1] == lane % 64
        hits = hits + jnp.where(same, 1.0, 0.0)
        weights = weights + jnp.where(same, probs[:, k : k + 1], 0.0)
    earlier = jnp.where(iota((16, 16), 1) < iota((16, 16), 0), 1.0, 0.0).astype(BF)
    before = dot(earlier, hits.astype(BF)).astype(jnp.int32)
    slot = jnp.where(before == lane // 64, hits, 0.0)
    weights = weights * slot
    high = weights.astype(BF)
    rest = weights - high.astype(F32)
    middle = rest.astype(BF)
    low = (rest - middle.astype(F32)).astype(BF)
    spread = jnp.concatenate([slot.astype(BF), high, middle, low] * 4, axis=0)

    loads[2].wait()
    loads[3].wait()
    for q in range(4):
        quarter = slice(q * 512, (q + 1) * 512)
        parts[q * 64 : q * 64 + 16, :] = tok_v[:, quarter]
        for a in range(1, 4):
            parts[q * 64 + a * 16 : q * 64 + a * 16 + 16, :] = cot_v[:, quarter]

    for block in range(4):
        row = iota((256, 128), 0) + block * 256
        lane = iota((256, 128), 1)
        place = (row // 16 == lane % 64) & (row % 2 == lane // 64)
        picked = dot_nt(jnp.where(place, 1.0, 0.0).astype(BF), spread)
        row, col = iota((256, 256), 0), iota((256, 256), 1)
        right = (row // 4 % 4 == col // 64) & (
            (row // 2 % 2 == 1) == (col // 16 % 4 != 0)
        )
        picked = jnp.where(right, picked, 0.0)
        here = slice(block * 256, (block + 1) * 256)
        sel[here, :] = picked.astype(BF)
        send[here, :] = dot(sel[here, :], parts[...]).astype(BF)
        sel_t[:, here] = picked.T.astype(BF)

    pl.semaphore_wait(barrier, 64)

    def out_unit(group, i):
        d = ORDER[group * 16 + i]
        pltpu.make_async_remote_copy(
            send.at[chip_rows(*d)],
            got.at[pl.ds(group * 256 + i * 16, 16)],
            ss.at[group], rs.at[group], device_id=device(*d), device_id_type=MESH,
        ).start()

    def back_unit(group, i):
        dx, dy, dz = ORDER[group * 16 + i]
        pltpu.make_async_remote_copy(
            ret.at[pl.ds(group * 256 + i * 16, 16)],
            back.at[own],
            ss.at[4 + group], rs.at[4 + group],
            device_id=device(-dx, -dy, -dz), device_id_type=MESH,
        ).start()

    def all_units(unit, group):
        for i in range(16):
            if group * 16 + i != HOME:
                unit(group, i)

    def landed(group, ref, sem):
        whole = ref.at[pl.ds(0, 240 if group == HOME // 16 else 256)]
        pltpu.make_async_copy(whole, whole, sem).wait()

    for group in range(4):
        all_units(out_unit, group)
    own_out = pltpu.make_async_copy(send.at[own], got.at[pl.ds(HOME * 16, 16)], lsem.at[0])
    own_out.start()
    own_back = pltpu.make_async_copy(ret.at[pl.ds(HOME * 16, 16)], back.at[own], lsem.at[1])

    for load in loads[4:]:
        load.wait()

    def transpose(i, carry):
        at = pl.ds(pl.multiple_of(i * 256, 256), 256)
        wgu_t[:, at] = wgu[at, :].T
        wd_t[at, :] = wd[:, at].T
        return carry

    lax.fori_loop(0, 8, transpose, 0)

    def to_other(src, dst, sem):
        return pltpu.make_async_remote_copy(
            src, dst, ps.at[sem], pr.at[sem], device_id=other, device_id_type=MESH
        )

    def unpack(src, group, first):
        at = group * 256
        got_rows = dot(perm[...], src[at : at + 256, :]).astype(BF)
        to = slice(first, first + 32)
        for q in range(4):
            quarter = slice(q * 512, (q + 1) * 512)
            xt[to, quarter] = got_rows[q * 64 : q * 64 + 32, :]
            xc[to, quarter] = got_rows[q * 64 + 32 : q * 64 + 64, :]

    def share(group):
        at = pl.ds(group * 256, 256)
        return to_other(got.at[at], got_other.at[at], group)

    def arrive(chunk):
        groups = CHUNKS[chunk]
        for group in groups:
            landed(group, got, rs.at[group])
            if group == HOME // 16:
                own_out.wait()
            share(group).start()

    def open_own(chunk):
        groups = CHUNKS[chunk]
        for n, group in enumerate(groups):
            unpack(got, group, groups[0] * 64 + n * 32)

    def first_half(chunk):
        groups = CHUNKS[chunk]
        count = len(groups)
        first, half = groups[0] * 64, count * 32
        for n, group in enumerate(groups):
            share(group).wait_recv()
            unpack(got_other, group, first + half + n * 32)
        here = slice(first, first + 2 * half)
        gate_up = dot(xt[here, :], wgu[...])
        gate, up = gate_up[:, :384], gate_up[:, 384:]
        act_cot = dot(xc[here, :], wd_t[...])
        sig = jax.nn.sigmoid(gate)
        act[here, :] = (gate * sig * up).astype(BF)
        gu[here, :384] = (act_cot * up * sig * (1.0 + gate * (1.0 - sig))).astype(BF)
        gu[here, 384:] = (act_cot * gate * sig).astype(BF)

    def second_half(chunk):
        groups = CHUNKS[chunk]
        count = len(groups)
        first, half = groups[0] * 64, count * 32
        here = slice(first, first + 2 * half)
        base, size = groups[0] * 256, count * 64
        for pair in range(2):
            columns = slice(pair * 1024, (pair + 1) * 1024)
            cot_half = dot(gu[here, :], wgu_t[:, columns])
            out_half = dot(act[here, :], wd[:, columns])
            for q in (pair * 2, pair * 2 + 1):
                quarter = slice((q % 2) * 512, (q % 2) * 512 + 512)
                for n in range(count):
                    for a, value in enumerate((cot_half[:, quarter], out_half[:, quarter])):
                        to = base + q * size + n * 64 + a * 32
                        at = n * 32
                        mine[to : to + 32, :] = value[at : at + 32, :]
                        theirs[to : to + 32, :] = value[half + at : half + at + 32, :].astype(BF)
            piece = pl.ds(base + pair * 2 * size, 2 * size)
            to_other(theirs.at[piece], given.at[piece], 4 + chunk).start()

    def finish(chunk):
        groups = CHUNKS[chunk]
        count = len(groups)
        base, size = groups[0] * 256, count * 64
        whole = given.at[pl.ds(base, count * 256)]
        pltpu.make_async_copy(whole, whole, pr.at[4 + chunk]).wait()
        for n, group in enumerate(groups):
            pieces = []
            for q in range(4):
                at = base + q * size + n * 64
                pieces.append(
                    (mine[at : at + 64, :] + given[at : at + 64, :].astype(F32)).astype(BF)
                )
            back_rows = dot(perm_t[...], jnp.concatenate(pieces, axis=0)).astype(BF)
            ret[group * 256 : group * 256 + 256, :] = back_rows
        for group in groups:
            all_units(back_unit, group)
            if group == HOME // 16:
                own_back.start()

    def in_grads(i, carry):
        at = pl.ds(pl.multiple_of(i * 256, 256), 256)
        both = dot_tn(xt[:, at], gu[...])
        g_gate[at, :] = both[:, :384].astype(BF)
        g_up[at, :] = both[:, 384:].astype(BF)
        return carry

    def down_grads(i, carry):
        at = pl.ds(pl.multiple_of(i * 512, 512), 512)
        g_down[:, at] = dot_tn(act[...], xc[:, at]).astype(BF)
        return carry

    arrive(0)
    open_own(0)
    for chunk in range(len(CHUNKS)):
        first_half(chunk)
        if chunk:
            finish(chunk - 1)
        if chunk + 1 < len(CHUNKS):
            arrive(chunk + 1)
        second_half(chunk)
        if chunk + 1 < len(CHUNKS):
            open_own(chunk + 1)
    lax.fori_loop(0, 4, down_grads, 0)
    finish(len(CHUNKS) - 1)
    lax.fori_loop(0, 8, in_grads, 0)

    for group in range(4):
        landed(group, back, rs.at[4 + group])
        landed(group, send, ss.at[group])
        landed(group, ret, ss.at[4 + group])
        share(group).wait_send()
    for chunk, groups in enumerate(CHUNKS):
        whole = theirs.at[pl.ds(0, len(groups) * 256)]
        pltpu.make_async_copy(whole, whole, ps.at[4 + chunk]).wait()
    own_back.wait()


def combine(
    back, sel_t, g_gate, g_up, g_down,
    o_mixed, o_token, o_gate, o_up, o_down, mixed, token_grad, sems,
):
    stores = [
        pltpu.make_async_copy(src, dst, sems.at[n])
        for n, (src, dst) in enumerate((
            (g_gate, o_gate.at[0]), (g_up, o_up.at[0]), (g_down, o_down.at[0]),
            (mixed, o_mixed), (token_grad, o_token),
        ))
    ]
    for store in stores[:3]:
        store.start()
    both = dot(sel_t[...], back[...])
    for q in range(4):
        quarter = slice(q * 512, (q + 1) * 512)
        at = q * 64
        token_grad[:, quarter] = both[at : at + 16, :].astype(BF)
        mixed[:, quarter] = (
            both[at + 16 : at + 32, :] + both[at + 32 : at + 48, :] + both[at + 48 : at + 64, :]
        ).astype(BF)
    for store in stores[3:]:
        store.start()
    for store in stores:
        store.wait()


def body(tokens, route, probs, cotangent, gate_weight, up_weight, down_weight):
    hbm_spec = pl.BlockSpec(memory_space=pltpu.HBM)
    vmem_spec = pl.BlockSpec(memory_space=pltpu.VMEM)
    kept = pl.pallas_call(
        exchange,
        name="exchange",
        out_shape=[
            pltpu.VMEM((1024, 512), BF),
            pltpu.VMEM((256, 1024), BF),
            pltpu.VMEM((2048, 384), BF),
            pltpu.VMEM((2048, 384), BF),
            pltpu.VMEM((384, 2048), BF),
        ],
        in_specs=[hbm_spec] * 7,
        out_specs=[vmem_spec] * 5,
        scratch_shapes=[
            pltpu.VMEM((8, 16), jnp.int32),
            pltpu.VMEM((8, 16), F32),
            pltpu.VMEM((16, 2048), BF),
            pltpu.VMEM((16, 2048), BF),
            pltpu.VMEM((2048, 768), BF),
            pltpu.VMEM((384, 2048), BF),
            pltpu.VMEM((768, 2048), BF),
            pltpu.VMEM((2048, 384), BF),
            pltpu.VMEM((256, 256), BF),
            pltpu.VMEM((256, 256), BF),
            pltpu.VMEM((1024, 256), BF),
            pltpu.VMEM((256, 512), BF),
            pltpu.VMEM((1024, 512), BF),
            pltpu.VMEM((1024, 512), BF),
            pltpu.VMEM((1024, 512), BF),
            pltpu.VMEM((256, 2048), BF),
            pltpu.VMEM((256, 2048), BF),
            pltpu.VMEM((256, 384), BF),
            pltpu.VMEM((256, 768), BF),
            pltpu.VMEM((1024, 512), F32),
            pltpu.VMEM((1024, 512), BF),
            pltpu.VMEM((1024, 512), BF),
            pltpu.VMEM((1024, 512), BF),
            pltpu.SemaphoreType.DMA((7,)),
            pltpu.SemaphoreType.DMA((8,)),
            pltpu.SemaphoreType.DMA((8,)),
            pltpu.SemaphoreType.DMA((2,)),
            pltpu.SemaphoreType.DMA((8,)),
            pltpu.SemaphoreType.DMA((8,)),
        ],
        compiler_params=pltpu.CompilerParams(
            collective_id=0, has_side_effects=True, vmem_limit_bytes=60751872
        ),
    )(route.T, probs.T, tokens, cotangent, gate_weight, up_weight, down_weight)
    return pl.pallas_call(
        combine,
        name="combine",
        out_shape=[
            jax.ShapeDtypeStruct(tokens.shape, BF),
            jax.ShapeDtypeStruct(tokens.shape, BF),
            jax.ShapeDtypeStruct(gate_weight.shape, BF),
            jax.ShapeDtypeStruct(up_weight.shape, BF),
            jax.ShapeDtypeStruct(down_weight.shape, BF),
        ],
        in_specs=[vmem_spec] * 5,
        out_specs=[hbm_spec] * 5,
        scratch_shapes=[
            pltpu.VMEM(tokens.shape, BF),
            pltpu.VMEM(tokens.shape, BF),
            pltpu.SemaphoreType.DMA((5,)),
        ],
        compiler_params=pltpu.CompilerParams(vmem_limit_bytes=16 << 20),
    )(*kept)


def solution(mesh):
    rows = P(("dp", "expert"), None)
    slices = P(("dp", "expert"), None, None)
    return jax.shard_map(
        body,
        mesh=mesh,
        in_specs=(rows, rows, rows, rows, slices, slices, slices),
        out_specs=(rows, rows, slices, slices, slices),
        check_vma=False,
    )
```
